32 devices in a mesh: dp: 4 (over z), tensor: 8 (over y, x, core).
Axes of the slice: x: 2, y: 2, z: 4, core: 2. Of those that a mesh axis runs over, the one named last changes fastest.
Arguments:
- block_input: bfloat16 [1, 12544, 512], P(None, ('dp', 'tensor')), may hold values from -6 to 6
- out_cotangent: bfloat16 [1, 12544, 512], P(None, ('dp', 'tensor')), may hold values from -6 to 6
- live_images: int32 [4], P('dp'), may hold values from 4 to 16, as said below
- width_params: bfloat16 [6, 512], P(None, 'dp'), may hold values from -4 to 4
- w_qkv: bfloat16 [512, 1536], P('dp', 'tensor'), may hold values from -0.25 to 0.25
- qv_bias: bfloat16 [2, 8, 64], P(None, 'tensor', 'dp'), may hold values from -3 to 3
- bias_table: float32 [16, 169], P('tensor'), may hold values from -12 to 320
- w_proj: bfloat16 [512, 512], P('tensor', 'dp'), may hold values from -0.75 to 0.75
- fc1_w: bfloat16 [512, 2048], P('dp', 'tensor'), may hold values from -0.25 to 0.25
- fc1_bias: bfloat16 [8, 256], P('tensor', 'dp'), may hold values from -3 to 3
- fc2_w: bfloat16 [2048, 512], P('tensor', 'dp'), may hold values from -0.125 to 0.125
Outputs:
- block_output: bfloat16 [1, 12544, 512], P(None, ('dp', 'tensor'))
- input_grad: float32 [1, 12544, 512], P(None, ('dp', 'tensor'))
- g_width: float32 [6, 512], P(None, 'dp')
- g_qkv: float32 [512, 1536], P('dp', 'tensor')
- g_qv_bias: float32 [2, 8, 64], P(None, 'tensor', 'dp')
- g_table: float32 [16, 169], P('tensor')
- g_proj: float32 [512, 512], P('tensor', 'dp')
- g_fc1: float32 [512, 2048], P('dp', 'tensor')
- g_fc1_bias: float32 [8, 256], P('tensor', 'dp')
- g_fc2: float32 [2048, 512], P('tensor', 'dp')
The draws below stay inside these ranges and needn't reach their ends.
Inputs may be any that keep to these rules, and one draw needn't show every extreme that they name: Index d of dp has its first live_images[d] images live, counted over its 1 group in order; some index has all 16 images live.
All inputs are finite; a program needn't handle non-finite values.
Results may differ from the reference program's by a relative error of at most 0.014.
Values may be sent and summed in bfloat16 or wider, within the bound.
No kernel may reach another device: no remote copies, remote signals or barrier semaphores. Data moves between devices by JAX's collectives and lax.ppermute only.
A program may use at most 128 MiB of HBM per device.

```python
import jax
import jax.numpy as jnp
from jax import lax

D = 512
HEADS = 16
HEAD = 32
FF = 2048
WIN = 7
SIDE = 14
SHIFT = 3
MICRO = 1
IMG_MB = 16
TABLE = 169
ROWS = 12544
N_DP = 4
N_TENSOR = 8


def draw_live_images(key, part):
    largest = IMG_MB * MICRO
    counts = jax.random.randint(jax.random.fold_in(key, 11), (N_DP,), largest // 4, largest + 1)
    full_index = jax.random.randint(jax.random.fold_in(key, 12), (), 0, N_DP)
    return jnp.where(jnp.arange(N_DP) == full_index, largest, counts).astype(jnp.int32)


def draw_width_params(key, part):
    gain_rows = 1.0 + 0.4 * jax.random.uniform(jax.random.fold_in(key, 21), (6, D), jnp.float32, -1.0, 1.0)
    shifts = 0.5 * jax.random.normal(jax.random.fold_in(key, 22), (6, D), jnp.float32)
    shifts = jnp.clip(shifts, -3.0, 3.0)
    row_ids = jnp.arange(6)[:, None]
    chosen = jnp.where((row_ids == 0) | (row_ids == 2), gain_rows, shifts)
    return chosen.astype(jnp.bfloat16)


def draw_bias_table(key, part):
    values = 1.5 * jax.random.normal(jax.random.fold_in(key, 33), (HEADS, TABLE), jnp.float32)
    return jnp.clip(values, -9.0, 9.0)


def block_levels(own_key, dims, split, least, high):
    factor_of, own = 1.0, jax.random.fold_in(own_key, 6)
    for axis_at, blocks in split:
        draws = jnp.exp(jax.random.uniform(jax.random.fold_in(own, axis_at), (blocks,), jnp.float32, least / len(split), high / len(split)))
        factor_of = factor_of * jnp.repeat(draws, dims[axis_at] // blocks).reshape([-1 if axis == axis_at else 1 for axis in range(len(dims))])
    return factor_of


def gaussian(stream_key, shape, scale, limit, split=(), kind=jnp.bfloat16):
    values = jax.random.normal(stream_key, shape, jnp.float32) * scale
    if len(split) > 0:
        values = block_levels(stream_key, shape, split, -0.22, 0.18) * values
    return jnp.clip(values, min=-limit, max=limit).astype(kind)


def setup_inputs(seed: int = 0) -> dict:
    key_of = jax.random.split(jax.random.key(seed), 12)
    return {
        "block_input": gaussian(key_of[0], (MICRO, ROWS, D), 1.0, 6.0, ((1, 32),)),
        "out_cotangent": gaussian(key_of[1], (MICRO, ROWS, D), 1.0, 6.0, ((1, 32),)),
        "live_images": draw_live_images(jax.random.fold_in(key_of[11], 71), 0),
        "width_params": draw_width_params(jax.random.fold_in(key_of[11], 71), 0),
        "w_qkv": gaussian(key_of[4], (D, 3 * D), D ** -0.5, 0.25, ((0, 4), (1, 8))),
        "qv_bias": gaussian(key_of[5], (2, N_TENSOR, D // N_TENSOR), 0.5, 3.0, ((1, 8), (2, 4))),
        "bias_table": draw_bias_table(jax.random.fold_in(key_of[11], 71), 0),
        "w_proj": gaussian(key_of[7], (D, D), (D // 8) ** -0.5, 0.75, ((0, 8), (1, 4))),
        "fc1_w": gaussian(key_of[8], (D, FF), D ** -0.5, 0.25, ((0, 4), (1, 8))),
        "fc1_bias": gaussian(key_of[9], (N_TENSOR, FF // N_TENSOR), 0.5, 3.0, ((0, 8), (1, 4))),
        "fc2_w": gaussian(key_of[10], (FF, D), FF ** -0.5, 0.125, ((0, 8), (1, 4))),
    }


EPSILON = 1e-05
MASKED = -100.0

def window_tables():
    per_side = SIDE // WIN
    places = jnp.arange(SIDE)
    region_band = jnp.where(places < SIDE - WIN, 0, jnp.where(places < SIDE - SHIFT, 1, 2))
    region = region_band[:, None] * 3 + region_band[None, :]
    region = region.reshape(per_side, WIN, per_side, WIN).transpose(0, 2, 1, 3).reshape(per_side * per_side, WIN * WIN)
    masking = jnp.where(region[:, :, None] == region[:, None, :], 0.0, MASKED).astype(jnp.float32)
    cell_ids = jnp.arange(WIN * WIN)
    rowpos = cell_ids // WIN
    colpos = cell_ids % WIN
    relative = (rowpos[:, None] - rowpos[None, :] + WIN - 1) * (2 * WIN - 1) + (colpos[:, None] - colpos[None, :] + WIN - 1)
    return (masking, relative.astype(jnp.int32))

def to_windows(grid_cells):
    image_count, features, per_side = (grid_cells.shape[0], grid_cells.shape[-1], SIDE // WIN)
    grid_cells = grid_cells.reshape(image_count, per_side, WIN, per_side, WIN, features).transpose(0, 1, 3, 2, 4, 5)
    return grid_cells.reshape(image_count * per_side * per_side, WIN * WIN, features)

def from_windows(windows, image_count):
    per_side, features = (SIDE // WIN, windows.shape[-1])
    grid_cells = windows.reshape(image_count, per_side, per_side, WIN, WIN, features).transpose(0, 1, 3, 2, 4, 5)
    return grid_cells.reshape(image_count, SIDE, SIDE, features)

def rows_to_windows(rows, image_count):
    grid_cells = jnp.roll(rows.reshape(image_count, SIDE, SIDE, rows.shape[-1]), (-SHIFT, -SHIFT), axis=(1, 2))
    return to_windows(grid_cells)

def windows_to_rows(windows, image_count):
    grid_cells = jnp.roll(from_windows(windows, image_count), (SHIFT, SHIFT), axis=(1, 2))
    return grid_cells.reshape(image_count * SIDE * SIDE, windows.shape[-1])

def normalize(value):
    row_mean = lax.optimization_barrier(jnp.mean(value, axis=-1, keepdims=True))
    centred = value - row_mean
    inv_std = lax.rsqrt(lax.optimization_barrier(jnp.mean(centred * centred, axis=-1, keepdims=True)) + EPSILON)
    return (centred * inv_std, inv_std)

def norm_back(grad, x_hat, inv_std):
    return inv_std * (grad - lax.optimization_barrier(jnp.mean(grad, axis=-1, keepdims=True)) - x_hat * lax.optimization_barrier(jnp.mean(grad * x_hat, axis=-1, keepdims=True)))

def gelu_parts(pre_act):
    normal_cdf = 0.5 * (1.0 + lax.erf(pre_act * 0.7071067811865476))
    normal_pdf = jnp.exp(-0.5 * pre_act * pre_act) * 0.3989422804014327
    return (pre_act * normal_cdf, normal_cdf + pre_act * normal_pdf)

def reference(block_input, out_cotangent, live_images, width_params, w_qkv, qv_bias, bias_table, w_proj, fc1_w, fc1_bias, fc2_w):
    masking, relative = window_tables()
    win_cells = WIN * WIN
    per_image = (SIDE // WIN) ** 2
    q_scale = HEAD ** (-0.5)
    params = width_params.astype(jnp.float32)
    qv_terms = qv_bias.astype(jnp.float32).reshape(2, HEADS, HEAD)
    first_bias = fc1_bias.astype(jnp.float32).reshape(FF)
    position = bias_table[:, relative]
    blocks = MICRO * N_DP
    tokens = IMG_MB * SIDE * SIDE
    x_blocks = block_input.reshape(blocks, tokens, D)
    dy_blocks = out_cotangent.reshape(blocks, tokens, D)
    owner_dp = jnp.arange(blocks) % N_DP
    first_image = jnp.arange(blocks) // N_DP * IMG_MB
    image_ids = jnp.arange(tokens) // (SIDE * SIDE)
    live_rows = (first_image[:, None] + image_ids[None, :] < live_images[owner_dp][:, None]).astype(jnp.float32)

    def one_block(totals, inputs):
        x_block, dy_block, live_block = inputs
        x_now = x_block.astype(jnp.float32)
        x_hat1, inv_std1 = normalize(x_now)
        normed1 = (x_hat1 * params[0] + params[1]).astype(jnp.bfloat16)
        qkv_rows = jnp.dot(normed1, w_qkv, preferred_element_type=jnp.float32).reshape(tokens, HEADS, 3, HEAD)
        query = (qkv_rows[:, :, 0] + qv_terms[0]) * q_scale
        value = qkv_rows[:, :, 2] + qv_terms[1]
        packed = jnp.stack([query, qkv_rows[:, :, 1], value], axis=2).astype(jnp.bfloat16)
        windows = rows_to_windows(packed.reshape(tokens, HEADS * 3 * HEAD), IMG_MB).reshape(-1, win_cells, HEADS, 3, HEAD)
        win_count = windows.shape[0]
        q_win = windows[:, :, :, 0].astype(jnp.float32)
        k_win = windows[:, :, :, 1].astype(jnp.float32)
        v_win = windows[:, :, :, 2].astype(jnp.float32)
        scores = jnp.einsum('wihd,wjhd->whij', q_win, k_win)
        scores = (scores.reshape(IMG_MB, per_image, HEADS, win_cells, win_cells) + position[None, None] + masking[None, :, None]).reshape(win_count, HEADS, win_cells, win_cells)
        peak = lax.optimization_barrier(jnp.max(scores, axis=-1, keepdims=True))
        raised = jnp.exp(scores - peak)
        probs = raised / lax.optimization_barrier(jnp.sum(raised, axis=-1, keepdims=True))
        probs_b = probs.astype(jnp.bfloat16).astype(jnp.float32)
        attended = jnp.einsum('whij,wjhd->wihd', probs_b, v_win).astype(jnp.bfloat16)
        heads_out = windows_to_rows(attended.reshape(win_count, win_cells, HEADS * HEAD), IMG_MB)
        x_mid = x_now + jnp.dot(heads_out, w_proj, preferred_element_type=jnp.float32) + params[4]
        x_hat2, inv_std2 = normalize(x_mid)
        normed2 = (x_hat2 * params[2] + params[3]).astype(jnp.bfloat16)
        pre_act = jnp.dot(normed2, fc1_w, preferred_element_type=jnp.float32) + first_bias
        activated, slope = gelu_parts(pre_act)
        activated_b = activated.astype(jnp.bfloat16)
        y_block = (x_mid + jnp.dot(activated_b, fc2_w, preferred_element_type=jnp.float32) + params[5]).astype(jnp.bfloat16)
        grad_y = dy_block.astype(jnp.float32) * live_block[:, None]
        grad_yb = grad_y.astype(jnp.bfloat16)
        g_fc2 = jnp.dot(activated_b.T, grad_yb, preferred_element_type=jnp.float32)
        grad_pre = jnp.dot(grad_yb, fc2_w.T, preferred_element_type=jnp.float32) * slope
        grad_pre_b = grad_pre.astype(jnp.bfloat16)
        g_fc1 = jnp.dot(normed2.T, grad_pre_b, preferred_element_type=jnp.float32)
        grad_n2 = jnp.dot(grad_pre_b, fc1_w.T, preferred_element_type=jnp.float32)
        grad_mid = grad_y + norm_back(grad_n2 * params[2], x_hat2, inv_std2)
        grad_mid_b = grad_mid.astype(jnp.bfloat16)
        g_proj = jnp.dot(heads_out.T, grad_mid_b, preferred_element_type=jnp.float32)
        grad_att = jnp.dot(grad_mid_b, w_proj.T, preferred_element_type=jnp.float32).astype(jnp.bfloat16)
        grad_win = rows_to_windows(grad_att, IMG_MB).reshape(win_count, win_cells, HEADS, HEAD).astype(jnp.float32)
        grad_v = jnp.einsum('whij,wihd->wjhd', probs_b, grad_win)
        grad_probs = jnp.einsum('wihd,wjhd->whij', grad_win, v_win)
        grad_s = probs * (grad_probs - lax.optimization_barrier(jnp.sum(probs * grad_probs, axis=-1, keepdims=True)))
        grad_sb = grad_s.astype(jnp.bfloat16).astype(jnp.float32)
        grad_q = jnp.einsum('whij,wjhd->wihd', grad_sb, k_win) * q_scale
        grad_k = jnp.einsum('whij,wihd->wjhd', grad_sb, q_win)
        table_terms = lax.optimization_barrier(jnp.sum(grad_s, axis=0))
        qv_grads = jnp.stack([lax.optimization_barrier(jnp.sum(grad_q, axis=(0, 1))), lax.optimization_barrier(jnp.sum(grad_v, axis=(0, 1)))])
        grad_pack = jnp.stack([grad_q, grad_k, grad_v], axis=3).astype(jnp.bfloat16)
        grad_rows = windows_to_rows(grad_pack.reshape(win_count, win_cells, HEADS * 3 * HEAD), IMG_MB)
        g_qkv = jnp.dot(normed1.T, grad_rows, preferred_element_type=jnp.float32)
        grad_n1 = jnp.dot(grad_rows, w_qkv.T, preferred_element_type=jnp.float32)
        grad_x = grad_mid + norm_back(grad_n1 * params[0], x_hat1, inv_std1)
        width_terms = jnp.stack([lax.optimization_barrier(jnp.sum(grad_n1 * x_hat1, axis=0)), lax.optimization_barrier(jnp.sum(grad_n1, axis=0)), lax.optimization_barrier(jnp.sum(grad_n2 * x_hat2, axis=0)), lax.optimization_barrier(jnp.sum(grad_n2, axis=0)), lax.optimization_barrier(jnp.sum(grad_mid, axis=0)), lax.optimization_barrier(jnp.sum(grad_y, axis=0))])
        terms = (width_terms, g_qkv, qv_grads, table_terms, g_proj, g_fc1, lax.optimization_barrier(jnp.sum(grad_pre, axis=0)), g_fc2)
        totals = tuple((total + term for total, term in zip(totals, terms)))
        return (totals, (y_block, grad_x))
    start = (jnp.zeros((6, D), jnp.float32), jnp.zeros((D, 3 * D), jnp.float32), jnp.zeros((2, HEADS, HEAD), jnp.float32), jnp.zeros((HEADS, win_cells, win_cells), jnp.float32), jnp.zeros((D, D), jnp.float32), jnp.zeros((D, FF), jnp.float32), jnp.zeros((FF,), jnp.float32), jnp.zeros((FF, D), jnp.float32))
    totals, outputs = lax.scan(one_block, start, (x_blocks, dy_blocks, live_rows))
    output_all = outputs[0].reshape(MICRO, N_DP * tokens, D)
    grad_all = outputs[1].reshape(MICRO, N_DP * tokens, D)
    g_width, g_qkv, g_qvb, table_terms, g_proj, g_fc1, g_b1, g_fc2 = totals
    g_table = jax.ops.segment_sum(table_terms.reshape(HEADS, -1).T, relative.reshape(-1), num_segments=TABLE).T
    return (output_all, grad_all, g_width, g_qkv, g_qvb.reshape(2, N_TENSOR, D // N_TENSOR), g_table, g_proj, g_fc1, g_b1.reshape(N_TENSOR, FF // N_TENSOR), g_fc2)
```

```python
import functools

import jax
import jax.numpy as jnp
import numpy as np
from jax import lax
from jax.experimental import pallas as pl
from jax.experimental.pallas import tpu as pltpu
from jax.sharding import PartitionSpec as P

HEAD = 32
WIN = 7
SIDE = 14
SHIFT = 3
TABLE = 169
EPSILON = 1e-05
MASKED = -100.0
NEVER = -1e30
SPAN = 2 * WIN - 1
CELL = 8
SLOT = 64
PAIR = 128
LANES = 128
SMALL = 32
F32 = jnp.float32
BF16 = jnp.bfloat16
AXES = ("dp", "tensor")


def window_constants(images):
    per_side = SIDE // WIN
    place = np.zeros((images * per_side * per_side * SLOT, images * SIDE * SIDE), np.float32)
    band = np.where(np.arange(SIDE) < SIDE - WIN, 0, np.where(np.arange(SIDE) < SIDE - SHIFT, 1, 2))
    mask = np.zeros((per_side, SLOT, PAIR), np.float32)
    select = np.zeros((LANES, PAIR), np.float32)
    region = np.full((per_side, per_side, SLOT), -1)
    for u in range(per_side):
        for v in range(per_side):
            for a in range(WIN):
                for b in range(WIN):
                    r, c = u * WIN + a, v * WIN + b
                    region[u, v, a * CELL + b] = band[r] * 3 + band[c]
                    source = ((r + SHIFT) % SIDE) * SIDE + (c + SHIFT) % SIDE
                    for image in range(images):
                        row = (image * per_side * per_side + u * per_side + v) * SLOT
                        place[row + a * CELL + b, image * SIDE * SIDE + source] = 1
                    select[a * SPAN + b, v * SLOT + a * CELL + b] = 1
    for u in range(per_side):
        for v in range(per_side):
            keys, queries = region[u, v][:, None], region[u, v][None, :]
            both = np.where((keys == queries) | (queries < 0), 0.0, MASKED)
            mask[u, :, v * SLOT : (v + 1) * SLOT] = np.where(keys < 0, NEVER, both)
    return place, mask, select


def dot(a, b):
    return lax.dot_general(a, b, (((1,), (0,)), ((), ())), preferred_element_type=F32)


def dot_nt(a, b):
    return lax.dot_general(a, b, (((1,), (1,)), ((), ())), preferred_element_type=F32)


def split3(value):
    high = value.astype(BF16)
    rest = value - high.astype(F32)
    middle = rest.astype(BF16)
    low = (rest - middle.astype(F32)).astype(BF16)
    return high, middle, low


def half_slot(t, me_t, tensor):
    rel = t ^ me_t
    colour = t & 1
    one, two = (rel >> 1) & 1, (rel >> 2) & 1
    first = one * (1 - colour) + two * colour
    return (rel >> 3) + (tensor // 8) * (first + 2 * (one + two - first))


def each_block(n_dp, tensor, own, other, body):
    me_d, me_t = lax.axis_index("dp"), lax.axis_index("tensor")
    for far, source in ((1, other), (0, own)):

        def step(k, carry, far=far, source=source):
            t = 2 * k + (far ^ (me_t & 1))
            start = n_dp * half_slot(t, me_t, tensor)
            body(far, source, t, [start + (d ^ me_d) for d in range(n_dp)], start)
            return carry

        lax.fori_loop(0, tensor // 2, step, 0)


def normalize(value):
    mean = jnp.mean(value, axis=-1, keepdims=True)
    centred = value - mean
    inv_std = lax.rsqrt(jnp.mean(centred * centred, axis=-1, keepdims=True) + EPSILON)
    return centred * inv_std, inv_std


def norm_back(grad, x_hat, inv_std):
    return inv_std * (
        grad
        - jnp.mean(grad, axis=-1, keepdims=True)
        - x_hat * jnp.mean(grad * x_hat, axis=-1, keepdims=True)
    )


def gelu_parts(pre_act):
    normal_cdf = 0.5 * (1.0 + lax.erf(pre_act * 0.7071067811865476))
    normal_pdf = jnp.exp(-0.5 * pre_act * pre_act) * 0.3989422804014327
    return pre_act * normal_cdf, normal_cdf + pre_act * normal_pdf


def head_masks(dtype):
    lane = lax.broadcasted_iota(jnp.int32, (1, 2 * LANES), 1)
    return [(((lane & (LANES - 1)) >> 5) == h).astype(F32).astype(dtype) for h in range(4)]


def stack_heads(pair, masks):
    both = jnp.concatenate([pair[:SLOT], pair[SLOT:]], axis=1)
    return jnp.concatenate([both * m for m in masks], axis=0)


def block_diag(pair):
    zero = jnp.zeros((SLOT, LANES), pair.dtype)
    return jnp.concatenate(
        [
            jnp.concatenate([pair[:SLOT], zero], axis=1),
            jnp.concatenate([zero, pair[SLOT:]], axis=1),
        ],
        axis=0,
    )


def pick(value):
    return jnp.concatenate([value[:SLOT, :LANES], value[SLOT:, LANES:]], axis=0)


def fold(value, masks):
    total = value[:SLOT] * masks[0]
    for h in range(1, 4):
        total = total + value[h * SLOT : (h + 1) * SLOT] * masks[h]
    return jnp.concatenate([total[:, :LANES], total[:, LANES:]], axis=0)


def identity():
    row = lax.broadcasted_iota(jnp.int32, (LANES, LANES), 0)
    column = lax.broadcasted_iota(jnp.int32, (LANES, LANES), 1)
    return (row == column).astype(F32).astype(BF16)


def pack_kernel(n_dp, tensor, wq, wp, width, qv, table, bias, out, rows):
    columns, lanes = wq.shape[1], wq.shape[0]
    me_d, me_t = lax.axis_index("dp"), lax.axis_index("tensor")
    eye_row = lax.broadcasted_iota(jnp.int32, (columns, columns), 0)
    eye_col = lax.broadcasted_iota(jnp.int32, (columns, columns), 1)
    eye = (eye_row == eye_col).astype(F32).astype(BF16)
    out[0:columns, :] = dot_nt(eye, wq[...]).astype(BF16)
    out[columns : columns + wp.shape[0], :] = wp[...]
    rows[...] = jnp.zeros_like(rows)
    rows[0:6, 0:lanes] = width[...].astype(F32)
    count = qv.shape[2]
    spread = jnp.zeros((8, LANES), F32)
    rows[6:7, 0:count] = qv[0].astype(F32)
    rows[7:8, 0:count] = qv[1].astype(F32)
    begin = lax.rem((me_t * n_dp + me_d) * count, lanes)
    rows[6:8, :] = pltpu.roll(rows[0:8, :], begin, 1)[6:8]
    count = bias.shape[1]
    rows[8:9, 0:count] = bias[...].astype(F32)
    begin = lax.rem((me_t * n_dp + me_d) * count, lanes)
    rows[8:16, :] = pltpu.roll(rows[8:16, :], begin, 1)
    heads, segments = table.shape[0], pl.cdiv(TABLE, lanes)
    for part, piece in enumerate(split3(table[...])):
        for h in range(heads):
            for s in range(segments):
                wide = min(lanes, TABLE - s * lanes)
                row = 9 + (part * heads + h) * segments + s
                rows[row : row + 1, 0:wide] = piece.astype(F32)[
                    h : h + 1, s * lanes : s * lanes + wide
                ]
    out[columns + wp.shape[0] :, :] = rows[:, 0:lanes].astype(BF16)


def forward_kernel(
    n_dp, tensor, x, own, other, place, select, mask,
    n1, q, k, v, wt, vec, probs, att,
    qv_blocks, tab_blocks, tab, spread, position,
):
    width, lanes = x.shape[1], own.shape[2]
    base = own.shape[1] - SMALL
    heads = width // HEAD
    own_heads, segments = heads // tensor, pl.cdiv(TABLE, lanes)
    me_d = lax.axis_index("dp")
    per_tensor, per_both = width // tensor, width // tensor // n_dp

    qv_blocks[...] = jnp.zeros_like(qv_blocks)
    tab_blocks[...] = jnp.zeros_like(tab_blocks)
    spread[...] = jnp.zeros_like(spread)

    def assemble(far, source, t, slots, start):
        for d, s in enumerate(slots):
            for h in range(own_heads):
                for j in range(3):
                    row = pl.multiple_of(j * width + (t * own_heads + h) * HEAD, HEAD)
                    wt[pl.ds(row, HEAD), d * lanes : (d + 1) * lanes] = source[
                        s, (h * 3 + j) * HEAD : (h * 3 + j + 1) * HEAD, :
                    ]
            small = source[s, base : base + SMALL, :].astype(F32)
            block = lax.div(t * per_tensor + d * per_both, lanes)
            qv_blocks[block] = qv_blocks[block] + small[0:8]
        small = source[start, base : base + SMALL, :].astype(F32)
        for h in range(own_heads):
            for s in range(segments):
                rows = [9 + (part * own_heads + h) * segments + s for part in range(3)]
                high, middle, low = [small[r : r + 1] for r in rows]
                tab_blocks[t * own_heads + h, 0:1, s * lanes : (s + 1) * lanes] = high + middle + low

    each_block(n_dp, tensor, own, other, assemble)
    for h in range(heads):
        tab[h : h + 1, :] = tab_blocks[h, 0:1, :]
    for d in range(n_dp):
        small = own[d ^ me_d, base : base + SMALL, :].astype(F32)
        vec[0:8, d * lanes : (d + 1) * lanes] = small[0:8]
    for b in range(width // lanes):
        vec[8:16, b * lanes : (b + 1) * lanes] = qv_blocks[b]

    x_hat, _ = normalize(dot(place[...], x[...]))
    n1[...] = (x_hat * vec[0:1, :] + vec[1:2, :]).astype(BF16)
    scale = HEAD ** (-0.5)
    q[...] = ((dot_nt(n1[...], wt[0:width, :]) + vec[14:15, :]) * scale).astype(BF16)
    k[...] = dot_nt(n1[...], wt[width : 2 * width, :]).astype(BF16)
    v[...] = (dot_nt(n1[...], wt[2 * width :, :]) + vec[15:16, :]).astype(BF16)

    for a in range(WIN):
        for b in range(WIN):
            shift = (SPAN * a + b - (TABLE - 1) // 2) % tab.shape[1]
            spread[:, a * CELL + b, :] = pltpu.roll(tab[...], shift, 1)[:, 0:LANES]
    for g in range(width // LANES):
        rows = spread[4 * g : 4 * g + 4].reshape(4 * SLOT, LANES)
        position[g] = sum(dot(piece, select[...]) for piece in split3(rows))

    masks, eye = head_masks(BF16), identity()

    def window_pair(p, carry):
        rows = pl.ds(pl.multiple_of(p * PAIR, PAIR), PAIR)
        away = mask[p & 1]
        for g in range(width // LANES):
            cols = slice(g * LANES, (g + 1) * LANES)
            scores = dot_nt(stack_heads(k[rows, cols], masks), block_diag(q[rows, cols]))
            scores = (scores + position[g]).reshape(4, SLOT, PAIR) + away[None]
            raised = jnp.exp(scores - jnp.max(scores, axis=1, keepdims=True))
            total = jnp.sum(raised, axis=1, keepdims=True)
            soft = (raised / total).reshape(4 * SLOT, PAIR)
            probs[p, g] = soft
            turned = dot_nt(eye, soft.astype(BF16)).astype(BF16)
            att[rows, cols] = pick(dot(turned, stack_heads(v[rows, cols], masks))).astype(BF16)
        return carry

    lax.fori_loop(0, x_hat.shape[0] // PAIR, window_pair, 0)


def middle_kernel(
    n_dp, tensor, live, x, gy, att, vec, own1, other1, own2, other2, own3, other3, place, back,
    y, g_mid, g_att, f1_send, f1_keep, f2_send, f2_keep, p_send, p_keep, sums, bias_sums,
    wp, n2, n2_t, gyb, gy_t, gn2, y_sum,
):
    width, lanes = x.shape[1], own1.shape[2]
    base = own1.shape[1] - SMALL
    per_tensor = width // tensor
    hidden = own2.shape[2]
    me_t = lax.axis_index("tensor")
    rows = n2.shape[0]
    image_rows = (SIDE // WIN) ** 2 * SLOT

    def assemble(far, source, t, slots, start):
        for d, s in enumerate(slots):
            at = pl.multiple_of(t * per_tensor, per_tensor)
            wp[pl.ds(at, per_tensor), d * lanes : (d + 1) * lanes] = source[
                s, base - per_tensor : base, :
            ]

    each_block(n_dp, tensor, own1, other1, assemble)
    image = me_t * (rows // image_rows) + lax.broadcasted_iota(jnp.int32, (rows, 1), 0) // image_rows
    grad_y = dot(place[...], gy[...]) * (image < live[0]).astype(F32)
    gyb[...] = grad_y.astype(BF16)
    gy_t[...] = grad_y.T.astype(BF16)
    x_mid = dot(place[...], x[...]) + dot(att[...], wp[...]) + vec[4:5, :]
    x_hat, inv_std = normalize(x_mid)
    normed = x_hat * vec[2:3, :] + vec[3:4, :]
    n2[...] = normed.astype(BF16)
    n2_t[...] = normed.T.astype(BF16)
    gn2[...] = jnp.zeros_like(gn2)
    y_sum[...] = x_mid + vec[5:6, :]

    def chunk(far, source, t, slots, start):
        first, second = (other2, other3) if far else (own2, own3)
        f1_out, f2_out = (f1_send, f2_send) if far else (f1_keep, f2_keep)
        f1 = jnp.concatenate([first[s] for s in slots], axis=0)
        f2 = jnp.concatenate([second[s] for s in slots], axis=1)
        bias = []
        for segment in range(hidden // lanes):
            inside = [d for d in range(n_dp) if (d * (hidden // n_dp)) // lanes == segment]
            bias.append(
                sum(source[slots[d], base : base + SMALL, :].astype(F32)[8:9] for d in inside)
            )
        pre_act = dot(n2[...], f1) + jnp.concatenate(bias, axis=1)
        activated, slope = gelu_parts(pre_act)
        activated = activated.astype(BF16)
        y_sum[...] += dot(activated, f2)
        g_f2 = dot(gy_t[...], activated).astype(BF16)
        grad_pre = dot_nt(gyb[...], f2) * slope
        at = pl.multiple_of(t * hidden, hidden)
        bias_sums[0:1, pl.ds(at, hidden)] = jnp.sum(grad_pre, axis=0, keepdims=True)
        grad_pre = grad_pre.astype(BF16)
        gn2[...] += dot_nt(grad_pre, f1)
        g_f1 = dot(n2_t[...], grad_pre).astype(BF16)
        for d, s in enumerate(slots):
            f1_out[s] = g_f1[d * lanes : (d + 1) * lanes]
            f2_out[s] = g_f2[d * lanes : (d + 1) * lanes]

    each_block(n_dp, tensor, own1, other1, chunk)
    y[...] = dot(back[...], y_sum[...].astype(BF16)).astype(BF16)
    grad_n2 = gn2[...]
    grad_mid = grad_y + norm_back(grad_n2 * vec[2:3, :], x_hat, inv_std)
    g_mid[...] = grad_mid
    sums[...] = jnp.zeros_like(sums)
    sums[2:3, :] = jnp.sum(grad_n2 * x_hat, axis=0, keepdims=True)
    sums[3:4, :] = jnp.sum(grad_n2, axis=0, keepdims=True)
    sums[4:5, :] = jnp.sum(grad_mid, axis=0, keepdims=True)
    sums[5:6, :] = jnp.sum(grad_y, axis=0, keepdims=True)
    grad_mid = grad_mid.astype(BF16)
    g_att[...] = dot_nt(grad_mid, wp[...]).astype(BF16)
    wp[...] = dot(att[...].astype(F32).T.astype(BF16), grad_mid).astype(BF16)

    def deal(far, source, t, slots, start):
        out = p_send if far else p_keep
        for d, s in enumerate(slots):
            at = pl.multiple_of(t * per_tensor, per_tensor)
            out[s] = wp[pl.ds(at, per_tensor), d * lanes : (d + 1) * lanes]

    each_block(n_dp, tensor, own1, other1, deal)


def backward_kernel(
    n_dp, tensor, x, n1, q, k, v, probs, wt, vec, g_att, g_mid, sums, bias_sums,
    place, back, select,
    g_x, q_send, q_keep, small,
    g_rows, table_sum, g_w, tab, turned_t,
):
    width, lanes = x.shape[1], q_keep.shape[2]
    heads = width // HEAD
    own_heads, segments = heads // tensor, pl.cdiv(TABLE, lanes)
    hidden = bias_sums.shape[1] // tensor
    groups = width // LANES
    scale = HEAD ** (-0.5)
    masks, masks_f32, eye = head_masks(BF16), head_masks(F32), identity()
    table_sum[...] = jnp.zeros_like(table_sum)
    qv_zero = jnp.zeros((1, width), F32)

    def window_pair(p, carry):
        sum_q, sum_v = carry
        rows = pl.ds(pl.multiple_of(p * PAIR, PAIR), PAIR)
        parts_q, parts_v = [], []
        for g in range(groups):
            cols = slice(g * LANES, (g + 1) * LANES)
            values, keys = stack_heads(v[rows, cols], masks), stack_heads(k[rows, cols], masks)
            out_grad, queries = block_diag(g_att[rows, cols]), block_diag(q[rows, cols])
            soft = probs[p, g].reshape(4, SLOT, PAIR)
            g_probs = dot_nt(values, out_grad).reshape(4, SLOT, PAIR)
            inner = jnp.sum(soft * g_probs, axis=1, keepdims=True)
            g_score = (soft * (g_probs - inner)).reshape(4 * SLOT, PAIR)
            table_sum[g] += g_score
            g_score = g_score.astype(BF16)
            soft = soft.reshape(4 * SLOT, PAIR).astype(BF16)
            g_v = fold(dot(soft, out_grad), masks_f32)
            turned = dot_nt(eye, g_score).astype(BF16)
            g_q = pick(dot(turned, keys)) * scale
            g_k = fold(dot(g_score, queries), masks_f32)
            parts_q.append(jnp.sum(g_q, axis=0, keepdims=True))
            parts_v.append(jnp.sum(g_v, axis=0, keepdims=True))
            g_rows[rows, g * LANES : (g + 1) * LANES] = g_q.astype(BF16)
            g_rows[rows, width + g * LANES : width + (g + 1) * LANES] = g_k.astype(BF16)
            g_rows[rows, 2 * width + g * LANES : 2 * width + (g + 1) * LANES] = g_v.astype(BF16)
        return (
            sum_q + jnp.concatenate(parts_q, axis=1),
            sum_v + jnp.concatenate(parts_v, axis=1),
        )

    sum_q, sum_v = lax.fori_loop(0, n1.shape[0] // PAIR, window_pair, (qv_zero, qv_zero))

    for j in range(3 * groups):
        turned_t[j * LANES : (j + 1) * LANES, :] = dot_nt(
            eye, g_rows[:, j * LANES : (j + 1) * LANES]
        ).astype(BF16)
    g_w[...] = dot(turned_t[...], n1[...]).astype(BF16)

    def deal(far, source, t, slots, start):
        out = q_send if far else q_keep
        for d, s in enumerate(slots):
            for h in range(own_heads):
                for j in range(3):
                    row = pl.multiple_of(j * width + (t * own_heads + h) * HEAD, HEAD)
                    out[s, (h * 3 + j) * HEAD : (h * 3 + j + 1) * HEAD, :] = g_w[
                        pl.ds(row, HEAD), d * lanes : (d + 1) * lanes
                    ]

    each_block(n_dp, tensor, None, None, deal)

    x_hat, inv_std = normalize(dot(place[...], x[...]))
    grad_n1 = dot(g_rows[...], wt[...])
    grad_x = g_mid[...] + norm_back(grad_n1 * vec[0:1, :], x_hat, inv_std)
    g_x[...] = sum(dot(back[...], piece) for piece in split3(grad_x))
    sum_0 = jnp.sum(grad_n1 * x_hat, axis=0, keepdims=True)
    sum_1 = jnp.sum(grad_n1, axis=0, keepdims=True)

    tab[...] = jnp.zeros_like(tab)
    wide = tab.shape[1]
    pulled = []
    for g in range(groups):
        pieces = split3(table_sum[g])
        pulled.append(sum(dot_nt(piece, select[...]) for piece in pieces))
    for g in range(groups):
        table_sum[g] = pulled[g]
    zero = jnp.zeros((4, wide - LANES), F32)
    for a in range(WIN):
        for b in range(WIN):
            shift = ((TABLE - 1) // 2 - SPAN * a - b) % wide
            row = a * CELL + b
            picked = [
                jnp.concatenate([table_sum[g, h * SLOT + row : h * SLOT + row + 1, :] for h in range(4)], axis=0)
                for g in range(groups)
            ]
            both = jnp.concatenate(
                [jnp.concatenate([part, zero], axis=1) for part in picked], axis=0
            )
            tab[...] += pltpu.roll(both, shift, 1)

    me_d, me_t = lax.axis_index("dp"), lax.axis_index("tensor")
    small[...] = jnp.zeros_like(small)
    per_tensor, per_both = width // tensor, width // tensor // n_dp
    for t in range(tensor):
        start = n_dp * (half_slot(t, me_t, tensor) + (tensor // 2) * ((t ^ me_t) & 1))
        for d in range(n_dp):
            s = start + (d ^ me_d)
            cols = slice(d * lanes, (d + 1) * lanes)
            small[s, 0:1, :] = sum_0[:, cols]
            small[s, 1:2, :] = sum_1[:, cols]
            small[s, 2:6, :] = sums[2:6, cols]
            first = (t * per_tensor + d * per_both) // lanes * lanes
            small[s, 6:7, :] = sum_q[:, first : first + lanes]
            small[s, 7:8, :] = sum_v[:, first : first + lanes]
            first = (t * hidden + d * (hidden // n_dp)) // lanes * lanes
            small[s, 8:9, :] = bias_sums[0:1, first : first + lanes]
            for h in range(own_heads):
                for j in range(segments):
                    row = 9 + h * segments + j
                    small[s, row : row + 1, :] = tab[
                        t * own_heads + h : t * own_heads + h + 1, j * lanes : (j + 1) * lanes
                    ]


def make_swaps(n_dp, tensor):
    total = n_dp * tensor

    def swap(value, mask_of):
        return lax.ppermute(value, AXES, [(i, i ^ mask_of(i)) for i in range(total)])

    def first(i):
        return 4 if i & 1 else 2

    def second(i):
        return 2 if i & 1 else 4

    plain = [(lambda i, bit=bit: 1 << bit) for bit in range(tensor.bit_length() - 2, 2, -1)]
    middle = plain + [first, second]
    core = lambda i: 1
    along = [(lambda i, far=far: far * tensor) for far in range(1, n_dp)]
    return swap, along, middle, core


def gather(block, swaps):
    swap, along, middle, core = swaps
    held = jnp.stack([block] + [swap(block, mask) for mask in along])
    for mask in middle:
        held = jnp.concatenate([held, swap(held, mask)], axis=0)
    return held, swap(held, core)


def add(a, b):
    return (a.astype(F32) + b.astype(F32)).astype(a.dtype)


def scatter(send, keep, swaps):
    swap, along, middle, core = swaps
    held = add(keep, swap(send, core))
    for mask in reversed(middle):
        half = held.shape[0] // 2
        held = add(held[:half], swap(held[half:], mask))
    total = held[0].astype(F32)
    for far, mask in enumerate(along):
        total = total + swap(held[far + 1], mask).astype(F32)
    return total


def call(kernel, outs, scratch, args, flops, limit=48 << 20):
    vmem = pl.BlockSpec(memory_space=pltpu.VMEM)
    smem = pl.BlockSpec(memory_space=pltpu.SMEM)
    return pl.pallas_call(
        kernel,
        out_shape=[jax.ShapeDtypeStruct(shape, dtype) for shape, dtype in outs],
        in_specs=[smem if a.dtype == jnp.int32 else vmem for a in args],
        out_specs=[vmem] * len(outs),
        scratch_shapes=[pltpu.VMEM(shape, dtype) for shape, dtype in scratch],
        compiler_params=pltpu.CompilerParams(vmem_limit_bytes=limit),
        cost_estimate=pl.CostEstimate(flops=flops, bytes_accessed=1 << 20, transcendentals=0),
    )(*args)


def per_device(
    block_input,
    out_cotangent,
    live_images,
    width_params,
    w_qkv,
    qv_bias,
    bias_table,
    w_proj,
    fc1_w,
    fc1_bias,
    fc2_w,
):
    n_dp, tensor = lax.axis_size("dp"), lax.axis_size("tensor")
    swaps = make_swaps(n_dp, tensor)
    _, rows_dev, width = block_input.shape
    images = rows_dev // (SIDE * SIDE)
    rows = images * (SIDE // WIN) ** 2 * SLOT
    lanes, columns = w_qkv.shape
    per_tensor = w_proj.shape[0]
    hidden = fc1_w.shape[1]
    heads = width // HEAD
    groups = width // LANES
    half = n_dp * tensor // 2
    place_np, mask_np, select_np = window_constants(images)
    place, back = jnp.asarray(place_np, BF16), jnp.asarray(place_np.T, BF16)
    mask, select = jnp.asarray(mask_np), jnp.asarray(select_np, BF16)
    bind = lambda kernel: functools.partial(kernel, n_dp, tensor)
    x, gy = block_input[0], out_cotangent[0]

    (packed,) = call(
        bind(pack_kernel),
        [((columns + per_tensor + SMALL, lanes), BF16)],
        [((SMALL, LANES), F32)],
        [w_qkv, w_proj, width_params, qv_bias, bias_table, fc1_bias],
        1 << 24,
    )
    own1, other1 = gather(packed, swaps)
    own2, other2 = gather(fc1_w, swaps)
    own3, other3 = gather(fc2_w, swaps)

    wide = 2 * LANES
    n1, q, k, v, wt, vec, probs, att = call(
        bind(forward_kernel),
        [
            ((rows, width), BF16),
            ((rows, width), BF16),
            ((rows, width), BF16),
            ((rows, width), BF16),
            ((3 * width, width), BF16),
            ((16, width), F32),
            ((rows // PAIR, groups, 4 * SLOT, PAIR), F32),
            ((rows, width), BF16),
        ],
        [
            ((width // lanes, 8, lanes), F32),
            ((heads, 8, wide), F32),
            ((heads, wide), F32),
            ((heads, SLOT, LANES), F32),
            ((groups, 4 * SLOT, PAIR), F32),
        ],
        [x, own1, other1, place, select, mask],
        4 << 30,
    )

    outs = [
        ((rows_dev, width), BF16),
        ((rows, width), F32),
        ((rows, width), BF16),
        ((half, lanes, hidden), BF16),
        ((half, lanes, hidden), BF16),
        ((half, lanes, hidden), BF16),
        ((half, lanes, hidden), BF16),
        ((half, per_tensor, lanes), BF16),
        ((half, per_tensor, lanes), BF16),
        ((8, width), F32),
        ((8, hidden * tensor), F32),
    ]
    y, g_mid, g_att, f1_send, f1_keep, f2_send, f2_keep, p_send, p_keep, sums, bias_sums = call(
        bind(middle_kernel),
        outs,
        [
            ((width, width), BF16),
            ((rows, width), BF16),
            ((width, rows), BF16),
            ((rows, width), BF16),
            ((width, rows), BF16),
            ((rows, width), F32),
            ((rows, width), F32),
        ],
        [live_images, x, gy, att, vec, own1, other1, own2, other2, own3, other3, place, back],
        8 << 30,
    )
    g_fc2 = scatter(f2_send, f2_keep, swaps)
    g_fc1 = scatter(f1_send, f1_keep, swaps)
    g_proj = scatter(p_send, p_keep, swaps)

    g_x, q_send, q_keep, small = call(
        bind(backward_kernel),
        [
            ((rows_dev, width), F32),
            ((half, columns, lanes), BF16),
            ((half, columns, lanes), BF16),
            ((2 * half, 16, lanes), F32),
        ],
        [
            ((rows, 3 * width), BF16),
            ((groups, 4 * SLOT, PAIR), F32),
            ((3 * width, width), BF16),
            ((heads, wide), F32),
            ((3 * width, rows), BF16),
        ],
        [x, n1, q, k, v, probs, wt, vec, g_att, g_mid, sums, bias_sums, place, back, select],
        6 << 30,
    )
    g_qkv = scatter(q_send, q_keep, swaps)
    small = scatter(small[half:], small[:half], swaps)

    me = lax.axis_index("tensor") * n_dp + lax.axis_index("dp")
    count = qv_bias.shape[2]
    g_qv = lax.dynamic_slice(small[6:8], (0, lax.rem(me * count, lanes)), (2, count))
    count = fc1_bias.shape[1]
    g_b1 = lax.dynamic_slice(small[8:9], (0, lax.rem(me * count, lanes)), (1, count))
    own_heads = bias_table.shape[0]
    g_table = small[9 : 9 + own_heads * pl.cdiv(TABLE, lanes)].reshape(own_heads, -1)[:, :TABLE]
    return (
        y[None],
        g_x[None],
        small[0:6],
        g_qkv.T,
        g_qv[:, None, :],
        g_table,
        g_proj,
        g_fc1,
        g_b1,
        g_fc2.T,
    )


def solution(mesh):
    rows = P(None, AXES, None)
    placed = (
        rows,
        rows,
        P("dp"),
        P(None, "dp"),
        P("dp", "tensor"),
        P(None, "tensor", "dp"),
        P("tensor", None),
        P("tensor", "dp"),
        P("dp", "tensor"),
        P("tensor", "dp"),
        P("tensor", "dp"),
    )
    return jax.shard_map(
        per_device,
        mesh=mesh,
        in_specs=placed,
        out_specs=(rows, rows) + placed[3:],
        check_vma=False,
    )
```
